32 devices in a mesh: clips: 2 (over y), tm: 4 (over z), rows: 4 (over x, core).
Axes of the slice: x: 2, y: 2, z: 4, core: 2. Of those that a mesh axis runs over, the one named last changes fastest.
Arguments:
- latents: bfloat16 [32, 8, 192, 128], P(('clips', 'tm'), 'rows'), parts along dimension 0, may hold values from -6 to 6
- conv_weight: bfloat16 [3, 27, 192, 192], replicated, may hold values from -0.078125 to 0.078125
- norm_gains: float32 [3, 192], replicated, may hold values from 0.5 to 1.5
- biases: float32 [3, 192], replicated, may hold values from -3 to 3
Outputs:
- decoded: bfloat16 [32, 8, 192, 128], P(('clips', 'tm'), 'rows'), parts along dimension 0
The draws below stay inside these ranges and needn't reach their ends.
There are 2 independent parts, one for each index of `clips`. The reference program is written for one: setup_inputs(seed, part) draws one part's arguments, and reference() takes and returns one part's arrays. A program takes and returns all parts, laid end to end along the dimension named above; an argument that names none is the same for every part. Nothing has to cross between parts.
All inputs are finite; a program needn't handle non-finite values.
Results may differ from the reference program's by a relative error of at most 0.011.
Values may be sent and summed in bfloat16 or wider, within the bound.
A program may use at most 64 MiB of HBM per device.

```python
import jax
import jax.numpy as jnp
from jax import lax

C = 192
W = 128
LAYERS = 3
FRAMES = 16
HEIGHT = 8


def block_levels(stream_key, dims, pieces, low, top_value):
    def one(axis_at, parts):
        draws = jax.random.uniform(jax.random.fold_in(jax.random.fold_in(stream_key, 6), axis_at), (parts,), jnp.float32, low / len(pieces), top_value / len(pieces))
        return jnp.repeat(jnp.exp(draws), dims[axis_at] // parts).reshape((-1,) + (1,) * (len(dims) - axis_at - 1))

    gain = one(*pieces[0])
    for cut in pieces[1:]:
        gain = gain * one(*cut)
    return gain


def normal_values(stream_key, shape, spread, bound, split=(), held_as=jnp.bfloat16):
    entries = jax.random.normal(stream_key, shape, jnp.float32) * spread
    if len(split) > 0:
        entries = block_levels(stream_key, shape, split, -0.22, 0.18) * entries
    return jnp.clip(entries, min=-bound, max=bound).astype(held_as)


def setup_inputs(seed: int = 0, part: int = 0) -> dict:
    streams_of = jax.random.split(jax.random.key(seed), 5)
    own_keys = jax.random.split(jax.random.fold_in(streams_of[4], part), 5)
    return {
        "latents": normal_values(own_keys[0], (FRAMES, HEIGHT, C, W), 1.0, 6.0, ((0, 4), (1, 4))),
        "conv_weight": normal_values(streams_of[1], (LAYERS, 27, C, C), (27 * C) ** -0.5, 0.078125),
        "norm_gains": jnp.clip(jax.random.uniform(streams_of[2], (LAYERS, C), jnp.float32, 0.5, 1.5), 0.5, 1.5),
        "biases": normal_values(streams_of[3], (LAYERS, C), 0.5, 3.0, (), jnp.float32),
    }


EPSILON = 1e-06

def activate(values, gain_row):
    widened = values.astype(jnp.float32)
    squares = lax.optimization_barrier(jnp.mean(widened * widened, axis=2, keepdims=True))
    normed = widened * lax.rsqrt(squares + EPSILON) * gain_row[None, None, :, None]
    return jax.nn.silu(normed).astype(jnp.bfloat16)

def one_layer(values, gain_row, weight, bias_row):
    rounded = activate(values, gain_row)
    padded = jnp.pad(lax.optimization_barrier(rounded).astype(jnp.float32), ((2, 0), (1, 1), (0, 0), (1, 1)))
    frames = values.shape[0]
    height = values.shape[1]
    columns = values.shape[3]
    total = jnp.zeros(values.shape, jnp.float32)
    for time_tap in range(3):
        for row_tap in range(3):
            for column_tap in range(3):
                window = padded[time_tap:time_tap + frames, row_tap:row_tap + height, :, column_tap:column_tap + columns]
                kernel = weight[9 * time_tap + 3 * row_tap + column_tap].astype(jnp.float32)
                total = total + jnp.einsum('oc,fhcw->fhow', kernel, window, precision=lax.Precision.HIGHEST)
    summed = values.astype(jnp.float32) + total + bias_row[None, None, :, None]
    return summed.astype(jnp.bfloat16)

def reference(latents, conv_weight, norm_gains, biases):
    values = latents
    for layer_index in range(LAYERS):
        values = one_layer(values, norm_gains[layer_index], conv_weight[layer_index], biases[layer_index])
    return values
```

```python
import functools

import jax
import jax.numpy as jnp
from jax import lax
from jax.experimental import pallas as pl
from jax.experimental.pallas import tpu as pltpu
from jax.sharding import PartitionSpec as P

EPSILON = 1e-06
MESH = pl.DeviceIdType.MESH
INNER, OUTER = 0, 1


def stack_kernel(
    layers, frames, rows_here, channels, columns,
    x_hbm, w_hbm, gains_hbm, biases_hbm, out_hbm,
    x_ref, w_raw, w_cat, acc, act, values, gains_ref, biases_ref, gain_col, bias_col,
    x_sem, w_sem, small_sem, out_sem,
    row_send, row_recv, tm_send, tm_recv, corner_send,
):
    tm, tm_count = lax.axis_index("tm"), lax.axis_size("tm")
    row, row_count = lax.axis_index("rows"), lax.axis_size("rows")
    odd = lax.rem(row, 2) == 1
    step = jnp.where(odd, 1, -1)
    inner, outer = row - step, row + step
    has_prev, has_next = tm > 0, tm < tm_count - 1
    has_inner = inner < row_count
    has_outer = jnp.logical_and(outer >= 0, outer < row_count)
    last_row = rows_here
    edge_src = (jnp.where(odd, 1, last_row), jnp.where(odd, last_row, 1))
    edge_dst = (jnp.where(odd, last_row + 1, 0), jnp.where(odd, 0, last_row + 1))
    halo = (jnp.where(odd, 0, last_row + 1), jnp.where(odd, last_row + 1, 0))
    side_there = (has_inner, has_outer)
    side_target = ({"rows": inner}, {"rows": outer})

    def both(*conditions):
        return functools.reduce(jnp.logical_and, conditions)

    barrier = pltpu.get_barrier_semaphore()
    greetings = (
        (has_prev, {"tm": tm - 1}),
        (has_next, {"tm": tm + 1}),
        (has_inner, {"rows": inner}),
        (has_outer, {"rows": outer}),
        (both(has_prev, has_outer), {"tm": tm - 1, "rows": outer}),
        (both(has_next, has_outer), {"tm": tm + 1, "rows": outer}),
    )
    for there, target in greetings:
        @pl.when(there)
        def _(target=target):
            pl.semaphore_signal(barrier, inc=1, device_id=target, device_id_type=MESH)

    def x_copy(frame):
        return pltpu.make_async_copy(x_hbm.at[frame], x_ref.at[frame], x_sem.at[frame])

    def out_copy(frame):
        return pltpu.make_async_copy(values.at[frame], out_hbm.at[frame], out_sem.at[frame])

    def weights(layer):
        return pltpu.make_async_copy(w_hbm.at[layer], w_raw.at[layer], w_sem.at[layer])

    gains_copy = pltpu.make_async_copy(gains_hbm, gains_ref, small_sem.at[0])
    biases_copy = pltpu.make_async_copy(biases_hbm, biases_ref, small_sem.at[1])
    gains_copy.start()
    for frame in range(frames - 1, -1, -1):
        x_copy(frame).start()
    biases_copy.start()
    for layer in range(layers):
        weights(layer).start()

    def tm_row(j):
        return jnp.where(odd, 1 + j, last_row - j)

    def tm_copy(layer, at, j):
        return pltpu.make_async_remote_copy(
            src_ref=act.at[layer, frames + at, tm_row(j), 1],
            dst_ref=act.at[layer, at, tm_row(j), 1],
            send_sem=tm_send.at[layer, at, j],
            recv_sem=tm_recv.at[layer, at, j],
            device_id={"tm": tm + 1},
            device_id_type=MESH,
        )

    def corner_copy(layer, at):
        return pltpu.make_async_remote_copy(
            src_ref=act.at[layer, frames + at, edge_src[OUTER], 1],
            dst_ref=act.at[layer, at, edge_dst[OUTER], 1],
            send_sem=corner_send.at[layer, at],
            recv_sem=row_recv.at[layer, at, OUTER],
            device_id={"tm": tm + 1, "rows": outer},
            device_id_type=MESH,
        )

    def row_copy(layer, padded, side):
        return pltpu.make_async_remote_copy(
            src_ref=act.at[layer, padded, edge_src[side], 1],
            dst_ref=act.at[layer, padded, edge_dst[side], 1],
            send_sem=row_send.at[layer, padded, side],
            recv_sem=row_recv.at[layer, padded, side],
            device_id=side_target[side],
            device_id_type=MESH,
        )

    def corner_direct(layer, at):
        return True

    def send_frame(layer, frame):
        at = frame - (frames - 2)
        for side in (OUTER, INNER):
            @pl.when(side_there[side])
            def _(side=side):
                row_copy(layer, frame + 2, side).start()
        if at >= 0:
            @pl.when(has_next)
            def _():
                tm_copy(layer, at, 0).start()
            if corner_direct(layer, at):
                @pl.when(both(has_next, has_outer))
                def _():
                    corner_copy(layer, at).start()

            @pl.when(has_next)
            def _():
                for j in range(1, rows_here):
                    tm_copy(layer, at, j).start()

    def relay_inner(layer, at):
        @pl.when(has_prev)
        def _():
            tm_copy(layer, at, 0).wait_recv()

        @pl.when(both(has_prev, has_inner))
        def _():
            row_copy(layer, at, INNER).start()

    def arrive_tm(layer, at):
        @pl.when(has_prev)
        def _():
            for j in range(1, rows_here):
                tm_copy(layer, at, j).wait_recv()
        if not corner_direct(layer, at):
            @pl.when(both(has_prev, has_outer))
            def _():
                row_copy(layer, at, OUTER).start()
        for side in (INNER, OUTER):
            @pl.when(both(has_prev, side_there[side]))
            def _(side=side):
                row_copy(layer, at, side).wait_recv()

    def arrive_rows(layer, padded):
        for side in (INNER, OUTER):
            @pl.when(side_there[side])
            def _(side=side):
                row_copy(layer, padded, side).wait_recv()

    lane = lax.broadcasted_iota(jnp.int32, (channels, columns), 1)
    not_first, not_last = lane > 0, lane < columns - 1

    def shift(layer, padded, h):
        line = act[layer, padded, h, 1].astype(jnp.float32)
        left = jnp.where(not_first, pltpu.roll(line, 1, 1), 0.0)
        right = jnp.where(not_last, pltpu.roll(line, columns - 1, 1), 0.0)
        act[layer, padded, h, 0] = left.astype(jnp.bfloat16)
        act[layer, padded, h, 2] = right.astype(jnp.bfloat16)

    def activate(layer, frame, value):
        squares = jnp.mean(value * value, axis=1, keepdims=True)
        half = value * lax.rsqrt(squares + EPSILON) * gain_col[layer][None]
        act[layer, frame + 2, pl.ds(1, rows_here), 1] = (
            half + half * jnp.tanh(half)
        ).astype(jnp.bfloat16)

    def prepare(layer):
        weights(layer).wait()
        taps = w_raw.shape[1] // 3
        for a in range(3):
            for first in range(0, taps, 2):
                count = min(2, taps - first)
                tiles = [w_raw[layer, taps * a + first + n] for n in range(count)]
                block = jnp.concatenate(tiles, axis=1) if count > 1 else tiles[0]
                w_cat[layer, a, :, first * channels:(first + count) * channels] = block

    def columns_of(ref, layer):
        line = ref[pl.ds(layer, 1), :]
        return jnp.transpose(jnp.broadcast_to(line, (columns, channels)))

    gains_copy.wait()
    gain_col[0] = 0.5 * columns_of(gains_ref, 0)
    for frame in range(frames - 1, -1, -1):
        x_copy(frame).wait()
        activate(0, frame, x_ref[frame].astype(jnp.float32))
        if frame == frames - 1:
            greeted = sum(there.astype(jnp.int32) for there, _ in greetings)
            pl.semaphore_wait(barrier, greeted)
        send_frame(0, frame)

    biases_copy.wait()
    for layer in range(layers):
        if layer > 0:
            gain_col[layer] = 0.5 * columns_of(gains_ref, layer)
        bias_col[layer] = columns_of(biases_ref, layer)

    zero_line = jnp.zeros((channels, columns), jnp.bfloat16)

    @pl.when(jnp.logical_not(has_prev))
    def _():
        for layer in range(layers):
            for at in range(2):
                for h in range(rows_here + 2):
                    act[layer, at, h, 1] = zero_line

    for side in (INNER, OUTER):
        @pl.when(both(has_prev, jnp.logical_not(side_there[side])))
        def _(side=side):
            for layer in range(layers):
                for at in range(2):
                    act[layer, at, halo[side], 1] = zero_line

        @pl.when(jnp.logical_not(side_there[side]))
        def _(side=side):
            for layer in range(layers):
                for at in range(2, frames + 2):
                    act[layer, at, halo[side], 1] = zero_line

    for frame in range(frames):
        for h in range(1, rows_here + 1):
            shift(0, frame + 2, h)
    for layer in range(layers):
        prepare(layer)

    depth = 9 * channels

    def window(layer, padded):
        return jnp.concatenate(
            [act[layer, padded, h:h + 3].reshape(depth, columns) for h in range(rows_here)],
            axis=1,
        )

    started = set()

    def product(layer, frame, a):
        part = jnp.dot(
            w_cat[layer, a], window(layer, frame + a), preferred_element_type=jnp.float32
        )
        if (layer, frame) in started:
            part = acc[layer, frame] + part
        return part

    def accumulate(layer, frame, a):
        acc[layer, frame] = product(layer, frame, a)
        started.add((layer, frame))

    def finish(layer, frame, total):
        before = x_ref if layer == 0 else values
        results = []
        for h in range(rows_here):
            part = total[:, h * columns:(h + 1) * columns]
            summed = before[frame, h].astype(jnp.float32) + part + bias_col[layer]
            results.append(summed.astype(jnp.bfloat16))
        for h in range(rows_here):
            values[frame, h] = results[h]
        if layer < layers - 1:
            activate(layer + 1, frame, jnp.stack(results).astype(jnp.float32))

    def relay_before(layer, at):
        if at == 1:
            return frames - 3
        return -2 if layer == 0 else -1 if layer < layers - 1 else 0

    for layer in range(layers):
        for source in range(frames - 1, -3, -1):
            for at in (1, 0):
                if relay_before(layer, at) == source:
                    relay_inner(layer, at)
            padded = source + 2
            if source >= 0:
                arrive_rows(layer, padded)
                for h in (0, last_row + 1):
                    shift(layer, padded, h)
            else:
                arrive_tm(layer, padded)
                for h in range(rows_here + 2):
                    shift(layer, padded, h)
            done = source + 2
            if done < frames:
                finish(layer, done, product(layer, done, 0))
                if layer < layers - 1:
                    send_frame(layer + 1, done)
                    for h in range(1, rows_here + 1):
                        shift(layer + 1, done + 2, h)
                else:
                    out_copy(done).start()
            for frame, a in ((source + 1, 1), (source, 2)):
                if 0 <= frame < frames:
                    accumulate(layer, frame, a)

    for layer in range(layers):
        for at in range(2):
            @pl.when(has_next)
            def _(layer=layer, at=at):
                for j in range(rows_here):
                    tm_copy(layer, at, j).wait_send()

            if corner_direct(layer, at):
                @pl.when(both(has_next, has_outer))
                def _(layer=layer, at=at):
                    corner_copy(layer, at).wait_send()
            else:
                @pl.when(both(has_prev, has_outer))
                def _(layer=layer, at=at):
                    row_copy(layer, at, OUTER).wait_send()

            @pl.when(both(has_prev, has_inner))
            def _(layer=layer, at=at):
                row_copy(layer, at, INNER).wait_send()
        for side in (INNER, OUTER):
            @pl.when(side_there[side])
            def _(layer=layer, side=side):
                for padded in range(2, frames + 2):
                    row_copy(layer, padded, side).wait_send()
    for frame in range(frames):
        out_copy(frame).wait()


def on_device(latents, conv_weight, norm_gains, biases):
    frames, rows_here, channels, columns = latents.shape
    layers, taps = conv_weight.shape[:2]
    hbm = pl.BlockSpec(memory_space=pl.ANY)
    dma = pltpu.SemaphoreType.DMA
    return pl.pallas_call(
        functools.partial(stack_kernel, layers, frames, rows_here, channels, columns),
        out_shape=jax.ShapeDtypeStruct(latents.shape, latents.dtype),
        in_specs=[hbm, hbm, hbm, hbm],
        out_specs=hbm,
        scratch_shapes=[
            pltpu.VMEM(latents.shape, jnp.bfloat16),
            pltpu.VMEM((layers, taps, channels, channels), jnp.bfloat16),
            pltpu.VMEM((layers, 3, channels, 9 * channels), jnp.bfloat16),
            pltpu.VMEM((layers, frames, channels, rows_here * columns), jnp.float32),
            pltpu.VMEM((layers, frames + 2, rows_here + 2, 3, channels, columns), jnp.bfloat16),
            pltpu.VMEM(latents.shape, jnp.bfloat16),
            pltpu.VMEM((layers, channels), jnp.float32),
            pltpu.VMEM((layers, channels), jnp.float32),
            pltpu.VMEM((layers, channels, columns), jnp.float32),
            pltpu.VMEM((layers, channels, columns), jnp.float32),
            dma((frames,)),
            dma((layers,)),
            dma((2,)),
            dma((frames,)),
            dma((layers, frames + 2, 2)),
            dma((layers, frames + 2, 2)),
            dma((layers, 2, rows_here)),
            dma((layers, 2, rows_here)),
            dma((layers, 2)),
        ],
        compiler_params=pltpu.CompilerParams(
            collective_id=0, has_side_effects=True, vmem_limit_bytes=60 * 1024 * 1024
        ),
        name="conv_stack",
    )(latents, conv_weight, norm_gains, biases)


def solution(mesh):
    in_specs = (P(("clips", "tm"), "rows", None, None), P(), P(), P())
    out_specs = P(("clips", "tm"), "rows", None, None)
    return jax.shard_map(
        on_device, mesh=mesh, in_specs=in_specs, out_specs=out_specs, check_vma=False
    )
```

```python
import functools

import jax
import jax.numpy as jnp
from jax import lax
from jax.experimental import pallas as pl
from jax.experimental.pallas import tpu as pltpu
from jax.sharding import PartitionSpec as P

EPSILON = 1e-06
MESH = pl.DeviceIdType.MESH
INNER, OUTER = 0, 1


def stack_kernel(
    layers, frames, rows_here, channels, columns,
    x_hbm, w_hbm, gains_hbm, biases_hbm, out_ref,
    x_ref, w_raw, w_cat, acc, act, values, gains_ref, biases_ref, gain_col, bias_col,
    x_sem, w_sem, small_sem,
    row_send, row_recv, tm_send, tm_recv, corner_send,
):
    tm, tm_count = lax.axis_index("tm"), lax.axis_size("tm")
    row, row_count = lax.axis_index("rows"), lax.axis_size("rows")
    odd = lax.rem(row, 2) == 1
    step = jnp.where(odd, 1, -1)
    inner, outer = row - step, row + step
    has_prev, has_next = tm > 0, tm < tm_count - 1
    has_inner = inner < row_count
    has_outer = jnp.logical_and(outer >= 0, outer < row_count)
    last_row = rows_here
    edge_src = (jnp.where(odd, 1, last_row), jnp.where(odd, last_row, 1))
    edge_dst = (jnp.where(odd, last_row + 1, 0), jnp.where(odd, 0, last_row + 1))
    halo = (jnp.where(odd, 0, last_row + 1), jnp.where(odd, last_row + 1, 0))
    side_there = (has_inner, has_outer)
    side_target = ({"rows": inner}, {"rows": outer})

    def both(*conditions):
        return functools.reduce(jnp.logical_and, conditions)

    barrier = pltpu.get_barrier_semaphore()
    greetings = (
        (has_prev, {"tm": tm - 1}),
        (has_next, {"tm": tm + 1}),
        (has_inner, {"rows": inner}),
        (has_outer, {"rows": outer}),
        (both(has_prev, has_outer), {"tm": tm - 1, "rows": outer}),
        (both(has_next, has_outer), {"tm": tm + 1, "rows": outer}),
    )
    for there, target in greetings:
        @pl.when(there)
        def _(target=target):
            pl.semaphore_signal(barrier, inc=1, device_id=target, device_id_type=MESH)

    def x_copy(frame):
        return pltpu.make_async_copy(x_hbm.at[frame], x_ref.at[frame], x_sem.at[frame])

    def weights(layer):
        return pltpu.make_async_copy(w_hbm.at[layer], w_raw.at[layer], w_sem.at[layer])

    gains_copy = pltpu.make_async_copy(gains_hbm, gains_ref, small_sem.at[0])
    biases_copy = pltpu.make_async_copy(biases_hbm, biases_ref, small_sem.at[1])
    gains_copy.start()
    for frame in range(frames - 1, -1, -1):
        x_copy(frame).start()
    biases_copy.start()
    for layer in range(layers):
        weights(layer).start()

    def tm_row(j):
        return jnp.where(odd, 1 + j, last_row - j)

    def tm_copy(layer, at, j):
        return pltpu.make_async_remote_copy(
            src_ref=act.at[layer, frames + at, tm_row(j), 1],
            dst_ref=act.at[layer, at, tm_row(j), 1],
            send_sem=tm_send.at[layer, at, j],
            recv_sem=tm_recv.at[layer, at, j],
            device_id={"tm": tm + 1},
            device_id_type=MESH,
        )

    def corner_copy(layer, at):
        return pltpu.make_async_remote_copy(
            src_ref=act.at[layer, frames + at, edge_src[OUTER], 1],
            dst_ref=act.at[layer, at, edge_dst[OUTER], 1],
            send_sem=corner_send.at[layer, at],
            recv_sem=row_recv.at[layer, at, OUTER],
            device_id={"tm": tm + 1, "rows": outer},
            device_id_type=MESH,
        )

    def row_copy(layer, padded, side):
        return pltpu.make_async_remote_copy(
            src_ref=act.at[layer, padded, edge_src[side], 1],
            dst_ref=act.at[layer, padded, edge_dst[side], 1],
            send_sem=row_send.at[layer, padded, side],
            recv_sem=row_recv.at[layer, padded, side],
            device_id=side_target[side],
            device_id_type=MESH,
        )

    def corner_direct(layer, at):
        return True

    def send_frame(layer, frame):
        at = frame - (frames - 2)
        for side in (OUTER, INNER):
            @pl.when(side_there[side])
            def _(side=side):
                row_copy(layer, frame + 2, side).start()
        if at >= 0:
            @pl.when(has_next)
            def _():
                tm_copy(layer, at, 0).start()
            if corner_direct(layer, at):
                @pl.when(both(has_next, has_outer))
                def _():
                    corner_copy(layer, at).start()

            @pl.when(has_next)
            def _():
                for j in range(1, rows_here):
                    tm_copy(layer, at, j).start()

    def relay(layer, at):
        direct = corner_direct(layer, at)

        @pl.when(has_prev)
        def _():
            for j in range(1 if direct else rows_here):
                tm_copy(layer, at, j).wait_recv()

        if not direct:
            @pl.when(both(has_prev, has_outer))
            def _():
                row_copy(layer, at, OUTER).start()

        @pl.when(both(has_prev, has_inner))
        def _():
            row_copy(layer, at, INNER).start()

    def arrive_tm(layer, at):
        if corner_direct(layer, at):
            @pl.when(has_prev)
            def _():
                for j in range(1, rows_here):
                    tm_copy(layer, at, j).wait_recv()
        for side in (INNER, OUTER):
            @pl.when(both(has_prev, side_there[side]))
            def _(side=side):
                row_copy(layer, at, side).wait_recv()

    def arrive_rows(layer, padded):
        for side in (INNER, OUTER):
            @pl.when(side_there[side])
            def _(side=side):
                row_copy(layer, padded, side).wait_recv()

    lane = lax.broadcasted_iota(jnp.int32, (channels, columns), 1)
    not_first, not_last = lane > 0, lane < columns - 1

    def shift(layer, padded, h):
        line = act[layer, padded, h, 1].astype(jnp.float32)
        left = jnp.where(not_first, pltpu.roll(line, 1, 1), 0.0)
        right = jnp.where(not_last, pltpu.roll(line, columns - 1, 1), 0.0)
        act[layer, padded, h, 0] = left.astype(jnp.bfloat16)
        act[layer, padded, h, 2] = right.astype(jnp.bfloat16)

    def activate(layer, frame, value):
        squares = jnp.mean(value * value, axis=1, keepdims=True)
        half = value * lax.rsqrt(squares + EPSILON) * gain_col[layer][None]
        act[layer, frame + 2, pl.ds(1, rows_here), 1] = (
            half + half * jnp.tanh(half)
        ).astype(jnp.bfloat16)

    def prepare(layer):
        weights(layer).wait()
        taps = w_raw.shape[1] // 3
        for a in range(3):
            for first in range(0, taps, 2):
                count = min(2, taps - first)
                tiles = [w_raw[layer, taps * a + first + n] for n in range(count)]
                block = jnp.concatenate(tiles, axis=1) if count > 1 else tiles[0]
                w_cat[layer, a, :, first * channels:(first + count) * channels] = block

    def columns_of(ref, layer):
        line = ref[pl.ds(layer, 1), :]
        return jnp.transpose(jnp.broadcast_to(line, (columns, channels)))

    gains_copy.wait()
    gain_col[0] = 0.5 * columns_of(gains_ref, 0)
    for frame in range(frames - 1, -1, -1):
        x_copy(frame).wait()
        activate(0, frame, x_ref[frame].astype(jnp.float32))
        if frame == frames - 1:
            greeted = sum(there.astype(jnp.int32) for there, _ in greetings)
            pl.semaphore_wait(barrier, greeted)
        send_frame(0, frame)

    biases_copy.wait()
    for layer in range(layers):
        if layer > 0:
            gain_col[layer] = 0.5 * columns_of(gains_ref, layer)
        bias_col[layer] = columns_of(biases_ref, layer)

    zero_line = jnp.zeros((channels, columns), jnp.bfloat16)

    @pl.when(jnp.logical_not(has_prev))
    def _():
        for layer in range(layers):
            for at in range(2):
                for h in range(rows_here + 2):
                    act[layer, at, h, 1] = zero_line

    for side in (INNER, OUTER):
        @pl.when(both(has_prev, jnp.logical_not(side_there[side])))
        def _(side=side):
            for layer in range(layers):
                for at in range(2):
                    act[layer, at, halo[side], 1] = zero_line

        @pl.when(jnp.logical_not(side_there[side]))
        def _(side=side):
            for layer in range(layers):
                for at in range(2, frames + 2):
                    act[layer, at, halo[side], 1] = zero_line

    for frame in range(frames):
        for h in range(1, rows_here + 1):
            shift(0, frame + 2, h)
    for layer in range(layers):
        prepare(layer)

    depth = 9 * channels

    def window(layer, padded):
        return jnp.concatenate(
            [act[layer, padded, h:h + 3].reshape(depth, columns) for h in range(rows_here)],
            axis=1,
        )

    started = set()

    def product(layer, frame, a):
        part = jnp.dot(
            w_cat[layer, a], window(layer, frame + a), preferred_element_type=jnp.float32
        )
        if (layer, frame) in started:
            part = acc[layer, frame] + part
        return part

    def accumulate(layer, frame, a):
        acc[layer, frame] = product(layer, frame, a)
        started.add((layer, frame))

    def finish(layer, frame, total):
        before = x_ref if layer == 0 else values
        results = []
        for h in range(rows_here):
            part = total[:, h * columns:(h + 1) * columns]
            summed = before[frame, h].astype(jnp.float32) + part + bias_col[layer]
            results.append(summed.astype(jnp.bfloat16))
        into = out_ref if layer == layers - 1 else values
        for h in range(rows_here):
            into[frame, h] = results[h]
        if layer < layers - 1:
            activate(layer + 1, frame, jnp.stack(results).astype(jnp.float32))

    def relay_before(layer, at):
        if at == 1:
            return frames - 3
        return -2 if layer == 0 else -1 if layer < layers - 1 else 0

    for layer in range(layers):
        for source in range(frames - 1, -3, -1):
            for at in (1, 0):
                if relay_before(layer, at) == source:
                    relay(layer, at)
            padded = source + 2
            if source >= 0:
                arrive_rows(layer, padded)
                for h in (0, last_row + 1):
                    shift(layer, padded, h)
            else:
                arrive_tm(layer, padded)
                for h in range(rows_here + 2):
                    shift(layer, padded, h)
            done = source + 2
            if done < frames:
                finish(layer, done, product(layer, done, 0))
            for frame, a in ((source + 1, 1), (source, 2)):
                if 0 <= frame < frames:
                    accumulate(layer, frame, a)
            if done < frames and layer < layers - 1:
                for h in range(1, rows_here + 1):
                    shift(layer + 1, done + 2, h)
                send_frame(layer + 1, done)

    for layer in range(layers):
        for at in range(2):
            @pl.when(has_next)
            def _(layer=layer, at=at):
                for j in range(rows_here):
                    tm_copy(layer, at, j).wait_send()

            if corner_direct(layer, at):
                @pl.when(both(has_next, has_outer))
                def _(layer=layer, at=at):
                    corner_copy(layer, at).wait_send()
            else:
                @pl.when(both(has_prev, has_outer))
                def _(layer=layer, at=at):
                    row_copy(layer, at, OUTER).wait_send()

            @pl.when(both(has_prev, has_inner))
            def _(layer=layer, at=at):
                row_copy(layer, at, INNER).wait_send()
        for side in (INNER, OUTER):
            @pl.when(side_there[side])
            def _(layer=layer, side=side):
                for padded in range(2, frames + 2):
                    row_copy(layer, padded, side).wait_send()


def on_device(latents, conv_weight, norm_gains, biases):
    frames, rows_here, channels, columns = latents.shape
    layers, taps = conv_weight.shape[:2]
    hbm = pl.BlockSpec(memory_space=pl.ANY)
    dma = pltpu.SemaphoreType.DMA
    return pl.pallas_call(
        functools.partial(stack_kernel, layers, frames, rows_here, channels, columns),
        out_shape=pltpu.VMEM(latents.shape, latents.dtype),
        in_specs=[hbm, hbm, hbm, hbm],
        out_specs=pl.BlockSpec(memory_space=pltpu.VMEM),
        scratch_shapes=[
            pltpu.VMEM(latents.shape, jnp.bfloat16),
            pltpu.VMEM((layers, taps, channels, channels), jnp.bfloat16),
            pltpu.VMEM((layers, 3, channels, 9 * channels), jnp.bfloat16),
            pltpu.VMEM((layers, frames, channels, rows_here * columns), jnp.float32),
            pltpu.VMEM((layers, frames + 2, rows_here + 2, 3, channels, columns), jnp.bfloat16),
            pltpu.VMEM(latents.shape, jnp.bfloat16),
            pltpu.VMEM((layers, channels), jnp.float32),
            pltpu.VMEM((layers, channels), jnp.float32),
            pltpu.VMEM((layers, channels, columns), jnp.float32),
            pltpu.VMEM((layers, channels, columns), jnp.float32),
            dma((frames,)),
            dma((layers,)),
            dma((2,)),
            dma((layers, frames + 2, 2)),
            dma((layers, frames + 2, 2)),
            dma((layers, 2, rows_here)),
            dma((layers, 2, rows_here)),
            dma((layers, 2)),
        ],
        compiler_params=pltpu.CompilerParams(
            collective_id=0, has_side_effects=True, vmem_limit_bytes=60 * 1024 * 1024
        ),
        name="conv_stack",
    )(latents, conv_weight, norm_gains, biases)


def solution(mesh):
    in_specs = (P(("clips", "tm"), "rows", None, None), P(), P(), P())
    out_specs = P(("clips", "tm"), "rows", None, None)
    return jax.shard_map(
        on_device, mesh=mesh, in_specs=in_specs, out_specs=out_specs, check_vma=False
    )
```

```python
import functools

import jax
import jax.numpy as jnp
from jax import lax
from jax.experimental import pallas as pl
from jax.experimental.pallas import tpu as pltpu
from jax.sharding import PartitionSpec as P

EPSILON = 1e-06
MESH = pl.DeviceIdType.MESH
INNER, OUTER = 0, 1
ROW_TAPS = (1, 0, 2)
CORNER_AFTER = ((1, 1), (1, 1), (1, 1))
RELAY_BEFORE = ((-1, 0), (0, 1), (-1, 2))
LAST_SOURCES = ((0, -1, -2), (0, -1, -2), (-1, 0, -2))
SENT_FIRST = ((), (), ())


def stack_kernel(
    layers, frames, rows_here, channels, columns,
    x_hbm, w_hbm, gains_hbm, biases_hbm, out_ref,
    x_ref, w_raw, w_cat, acc, act, values, gains_ref, biases_ref, gain_col, bias_col,
    x_sem, w_sem, small_sem,
    row_send, row_recv, tm_send, tm_recv, corner_send,
):
    tm, tm_count = lax.axis_index("tm"), lax.axis_size("tm")
    row, row_count = lax.axis_index("rows"), lax.axis_size("rows")
    odd = lax.rem(row, 2) == 1
    step = jnp.where(odd, 1, -1)
    inner, outer = row - step, row + step
    has_prev, has_next = tm > 0, tm < tm_count - 1
    has_inner = True if row_count % 2 == 0 else inner < row_count
    has_outer = jnp.logical_and(outer >= 0, outer < row_count)
    last_row = rows_here
    edge_src = (jnp.where(odd, 1, last_row), jnp.where(odd, last_row, 1))
    edge_dst = (jnp.where(odd, last_row + 1, 0), jnp.where(odd, 0, last_row + 1))
    halo = (jnp.where(odd, 0, last_row + 1), jnp.where(odd, last_row + 1, 0))
    side_there = (has_inner, has_outer)
    side_target = ({"rows": inner}, {"rows": outer})

    def both(*conditions):
        conditions = [there for there in conditions if there is not True]
        return functools.reduce(jnp.logical_and, conditions) if conditions else True

    def when(there):
        return (lambda body: body()) if there is True else pl.when(there)


    barrier = pltpu.get_barrier_semaphore()
    greetings = (
        (has_prev, {"tm": tm - 1}),
        (has_next, {"tm": tm + 1}),
        (has_inner, {"rows": inner}),
        (has_outer, {"rows": outer}),
        (both(has_prev, has_outer), {"tm": tm - 1, "rows": outer}),
        (both(has_next, has_outer), {"tm": tm + 1, "rows": outer}),
    )
    for there, target in greetings:
        @when(there)
        def _(target=target):
            pl.semaphore_signal(barrier, inc=1, device_id=target, device_id_type=MESH)

    def x_copy(frame):
        return pltpu.make_async_copy(x_hbm.at[frame], x_ref.at[frame], x_sem.at[frame])

    def weights(layer):
        return pltpu.make_async_copy(w_hbm.at[layer], w_raw.at[layer], w_sem.at[layer])

    gains_copy = pltpu.make_async_copy(gains_hbm, gains_ref, small_sem.at[0])
    biases_copy = pltpu.make_async_copy(biases_hbm, biases_ref, small_sem.at[1])
    gains_copy.start()
    for frame in range(frames - 1, -1, -1):
        x_copy(frame).start()
    biases_copy.start()
    for layer in range(layers):
        weights(layer).start()

    def tm_row(j):
        return jnp.where(odd, 1 + j, last_row - j)

    def tm_copy(layer, at, j):
        return pltpu.make_async_remote_copy(
            src_ref=act.at[layer, frames + at, tm_row(j), 1],
            dst_ref=act.at[layer, at, tm_row(j), 1],
            send_sem=tm_send.at[layer, at, j],
            recv_sem=tm_recv.at[layer, at, j],
            device_id={"tm": tm + 1},
            device_id_type=MESH,
        )

    def corner_copy(layer, at):
        return pltpu.make_async_remote_copy(
            src_ref=act.at[layer, frames + at, edge_src[OUTER], 1],
            dst_ref=act.at[layer, at, edge_dst[OUTER], 1],
            send_sem=corner_send.at[layer, at],
            recv_sem=row_recv.at[layer, at, OUTER],
            device_id={"tm": tm + 1, "rows": outer},
            device_id_type=MESH,
        )

    def row_copy(layer, padded, side):
        return pltpu.make_async_remote_copy(
            src_ref=act.at[layer, padded, edge_src[side], 1],
            dst_ref=act.at[layer, padded, edge_dst[side], 1],
            send_sem=row_send.at[layer, padded, side],
            recv_sem=row_recv.at[layer, padded, side],
            device_id=side_target[side],
            device_id_type=MESH,
        )

    def kind(layer):
        return 0 if layer == 0 else 2 if layer == layers - 1 else 1

    def send_frame(layer, frame):
        at = frame - (frames - 2)
        for side in (OUTER, INNER):
            @when(side_there[side])
            def _(side=side):
                row_copy(layer, frame + 2, side).start()
        if at >= 0:
            before = min(CORNER_AFTER[kind(layer)][at], rows_here)

            @pl.when(has_next)
            def _():
                for j in range(before):
                    tm_copy(layer, at, j).start()

            @when(both(has_next, has_outer))
            def _():
                corner_copy(layer, at).start()

            if before < rows_here:
                @pl.when(has_next)
                def _():
                    for j in range(before, rows_here):
                        tm_copy(layer, at, j).start()

    def relay(layer, at):
        @pl.when(has_prev)
        def _():
            tm_copy(layer, at, 0).wait_recv()

        @when(both(has_prev, has_inner))
        def _():
            row_copy(layer, at, INNER).start()

    def arrive_tm(layer, at):
        @pl.when(has_prev)
        def _():
            for j in range(1, rows_here):
                tm_copy(layer, at, j).wait_recv()
        for side in (INNER, OUTER):
            @when(both(has_prev, side_there[side]))
            def _(side=side):
                row_copy(layer, at, side).wait_recv()

    def arrive_rows(layer, padded):
        for side in (INNER, OUTER):
            @when(side_there[side])
            def _(side=side):
                row_copy(layer, padded, side).wait_recv()

    lane = lax.broadcasted_iota(jnp.int32, (channels, columns), 1)
    not_first, not_last = lane > 0, lane < columns - 1

    def shift(layer, padded, h):
        line = act[layer, padded, h, 1].astype(jnp.float32)
        left = jnp.where(not_first, pltpu.roll(line, 1, 1), 0.0)
        right = jnp.where(not_last, pltpu.roll(line, columns - 1, 1), 0.0)
        act[layer, padded, h, 0] = left.astype(jnp.bfloat16)
        act[layer, padded, h, 2] = right.astype(jnp.bfloat16)

    def activate(layer, frame, value):
        squares = jnp.mean(value * value, axis=1, keepdims=True)
        half = value * lax.rsqrt(squares + EPSILON) * gain_col[layer][None]
        act[layer, frame + 2, pl.ds(1, rows_here), 1] = (
            half + half * jnp.tanh(half)
        ).astype(jnp.bfloat16)

    def prepare(layer):
        weights(layer).wait()
        taps = w_raw.shape[1] // 3
        order = [3 * b + c for b in ROW_TAPS for c in range(3)]
        for a in range(3):
            for first in range(0, taps, 2):
                count = min(2, taps - first)
                tiles = [w_raw[layer, taps * a + order[first + n]] for n in range(count)]
                block = jnp.concatenate(tiles, axis=1) if count > 1 else tiles[0]
                w_cat[layer, a, :, first * channels:(first + count) * channels] = block

    def columns_of(ref, layer):
        line = ref[pl.ds(layer, 1), :]
        return jnp.transpose(jnp.broadcast_to(line, (columns, channels)))

    gains_copy.wait()
    gain_col[0] = 0.5 * columns_of(gains_ref, 0)
    for frame in range(frames - 1, -1, -1):
        x_copy(frame).wait()
        activate(0, frame, x_ref[frame].astype(jnp.float32))
        if frame == frames - 1:
            greeted = sum(jnp.int32(1) if there is True else there.astype(jnp.int32) for there, _ in greetings)
            pl.semaphore_wait(barrier, greeted)
        send_frame(0, frame)

    biases_copy.wait()
    for layer in range(layers):
        if layer > 0:
            gain_col[layer] = 0.5 * columns_of(gains_ref, layer)
        bias_col[layer] = columns_of(biases_ref, layer)

    zero_line = jnp.zeros((channels, columns), jnp.bfloat16)

    @pl.when(jnp.logical_not(has_prev))
    def _():
        for layer in range(layers):
            for at in range(2):
                for h in range(rows_here + 2):
                    act[layer, at, h, 1] = zero_line

    for side in (INNER, OUTER):
        if side_there[side] is True:
            continue

        @when(both(has_prev, jnp.logical_not(side_there[side])))
        def _(side=side):
            for layer in range(layers):
                for at in range(2):
                    act[layer, at, halo[side], 1] = zero_line

        @pl.when(jnp.logical_not(side_there[side]))
        def _(side=side):
            for layer in range(layers):
                for at in range(2, frames + 2):
                    act[layer, at, halo[side], 1] = zero_line

    for frame in range(frames):
        for h in range(1, rows_here + 1):
            shift(0, frame + 2, h)
    for layer in range(layers):
        prepare(layer)

    depth = 9 * channels

    def window(layer, padded):
        return jnp.concatenate(
            [
                jnp.concatenate(
                    [act[layer, padded, h + b].reshape(depth // 3, columns) for b in ROW_TAPS],
                    axis=0,
                )
                for h in range(rows_here)
            ],
            axis=1,
        )

    seen = {}

    def product(layer, frame, a):
        part = jnp.dot(
            w_cat[layer, a], window(layer, frame + a), preferred_element_type=jnp.float32
        )
        if seen.get((layer, frame), 0) > 0:
            part = acc[layer, frame] + part
        seen[layer, frame] = seen.get((layer, frame), 0) + 1
        return part

    def finish(layer, frame, total):
        before = x_ref if layer == 0 else values
        results = []
        for h in range(rows_here):
            part = total[:, h * columns:(h + 1) * columns]
            summed = before[frame, h].astype(jnp.float32) + part + bias_col[layer]
            results.append(summed.astype(jnp.bfloat16))
        into = out_ref if layer == layers - 1 else values
        for h in range(rows_here):
            into[frame, h] = results[h]
        if layer < layers - 1:
            activate(layer + 1, frame, jnp.stack(results).astype(jnp.float32))

    def pass_on(layer, frames_done):
        if layer < layers - 1:
            for frame in frames_done:
                for h in range(1, rows_here + 1):
                    shift(layer + 1, frame + 2, h)
                send_frame(layer + 1, frame)

    for layer in range(layers):
        order = list(range(frames - 1, 0, -1)) + list(LAST_SOURCES[kind(layer)])
        for source in order:
            for at in (1, 0):
                if min(RELAY_BEFORE[kind(layer)][at], frames - 1) == source:
                    relay(layer, at)
            padded = source + 2
            if source >= 0:
                arrive_rows(layer, padded)
                for h in (0, last_row + 1):
                    shift(layer, padded, h)
            else:
                arrive_tm(layer, padded)
                for h in range(rows_here + 2):
                    shift(layer, padded, h)
            touched = [f for f in (source + 2, source + 1, source) if 0 <= f < frames]
            done = [f for f in touched if seen.get((layer, f), 0) == 2]
            for frame in done:
                finish(layer, frame, product(layer, frame, padded - frame))
            apart = len(done) < len(touched) and source in SENT_FIRST[kind(layer)]
            if apart:
                pass_on(layer, done)
            for frame in touched:
                if frame not in done:
                    acc[layer, frame] = product(layer, frame, padded - frame)
            if not apart:
                pass_on(layer, done)

    for layer in range(layers):
        for at in range(2):
            @pl.when(has_next)
            def _(layer=layer, at=at):
                for j in range(rows_here):
                    tm_copy(layer, at, j).wait_send()

            @when(both(has_next, has_outer))
            def _(layer=layer, at=at):
                corner_copy(layer, at).wait_send()

            @when(both(has_prev, has_inner))
            def _(layer=layer, at=at):
                row_copy(layer, at, INNER).wait_send()
        for side in (INNER, OUTER):
            @when(side_there[side])
            def _(layer=layer, side=side):
                for padded in range(2, frames + 2):
                    row_copy(layer, padded, side).wait_send()


def on_device(latents, conv_weight, norm_gains, biases):
    frames, rows_here, channels, columns = latents.shape
    layers, taps = conv_weight.shape[:2]
    hbm = pl.BlockSpec(memory_space=pl.ANY)
    dma = pltpu.SemaphoreType.DMA
    return pl.pallas_call(
        functools.partial(stack_kernel, layers, frames, rows_here, channels, columns),
        out_shape=pltpu.VMEM(latents.shape, latents.dtype),
        in_specs=[hbm, hbm, hbm, hbm],
        out_specs=pl.BlockSpec(memory_space=pltpu.VMEM),
        scratch_shapes=[
            pltpu.VMEM(latents.shape, jnp.bfloat16),
            pltpu.VMEM((layers, taps, channels, channels), jnp.bfloat16),
            pltpu.VMEM((layers, 3, channels, 9 * channels), jnp.bfloat16),
            pltpu.VMEM((layers, frames, channels, rows_here * columns), jnp.float32),
            pltpu.VMEM((layers, frames + 2, rows_here + 2, 3, channels, columns), jnp.bfloat16),
            pltpu.VMEM(latents.shape, jnp.bfloat16),
            pltpu.VMEM((layers, channels), jnp.float32),
            pltpu.VMEM((layers, channels), jnp.float32),
            pltpu.VMEM((layers, channels, columns), jnp.float32),
            pltpu.VMEM((layers, channels, columns), jnp.float32),
            dma((frames,)),
            dma((layers,)),
            dma((2,)),
            dma((layers, frames + 2, 2)),
            dma((layers, frames + 2, 2)),
            dma((layers, 2, rows_here)),
            dma((layers, 2, rows_here)),
            dma((layers, 2)),
        ],
        compiler_params=pltpu.CompilerParams(
            collective_id=0, has_side_effects=True, vmem_limit_bytes=60 * 1024 * 1024
        ),
        name="conv_stack",
    )(latents, conv_weight, norm_gains, biases)


def solution(mesh):
    in_specs = (P(("clips", "tm"), "rows", None, None), P(), P(), P())
    out_specs = P(("clips", "tm"), "rows", None, None)
    return jax.shard_map(
        on_device, mesh=mesh, in_specs=in_specs, out_specs=out_specs, check_vma=False
    )
```

```python
import functools

import jax
import jax.numpy as jnp
from jax import lax
from jax.experimental import pallas as pl
from jax.experimental.pallas import tpu as pltpu
from jax.sharding import PartitionSpec as P

EPSILON = 1e-06
MESH = pl.DeviceIdType.MESH
INNER, OUTER = 0, 1
ROW_TAPS = (1, 0, 2)
CORNER_AFTER = ((1, 1), (1, 1), (1, 1))
RELAY_BEFORE = ((-1, 0), (0, 1), (-1, 2))
LAST_SOURCES = ((0, -1, -2), (0, -1, -2), (-1, 0, -2))
SENT_FIRST = ((), (), ())


def stack_kernel(
    layers, frames, rows_here, channels, columns,
    x_hbm, w_hbm, gains_hbm, biases_hbm, out_ref,
    x_ref, w_raw, w_cat, acc, act, values, gains_ref, biases_ref, gain_col, bias_col,
    x_sem, w_sem, small_sem,
    row_send, row_recv, tm_send, tm_recv, corner_send,
):
    tm, tm_count = lax.axis_index("tm"), lax.axis_size("tm")
    row, row_count = lax.axis_index("rows"), lax.axis_size("rows")
    odd = lax.rem(row, 2) == 1
    step = jnp.where(odd, 1, -1)
    inner, outer = row - step, row + step
    has_prev, has_next = tm > 0, tm < tm_count - 1
    has_inner = True if row_count % 2 == 0 else inner < row_count
    has_outer = jnp.logical_and(outer >= 0, outer < row_count)
    last_row = rows_here
    edge_src = (jnp.where(odd, 1, last_row), jnp.where(odd, last_row, 1))
    edge_dst = (jnp.where(odd, last_row + 1, 0), jnp.where(odd, 0, last_row + 1))
    halo = (jnp.where(odd, 0, last_row + 1), jnp.where(odd, last_row + 1, 0))
    side_there = (has_inner, has_outer)
    side_target = ({"rows": inner}, {"rows": outer})

    def both(*conditions):
        conditions = [there for there in conditions if there is not True]
        return functools.reduce(jnp.logical_and, conditions) if conditions else True

    def when(there):
        return (lambda body: body()) if there is True else pl.when(there)


    barrier = pltpu.get_barrier_semaphore()
    greetings = (
        (has_prev, {"tm": tm - 1}),
        (has_next, {"tm": tm + 1}),
        (has_inner, {"rows": inner}),
        (has_outer, {"rows": outer}),
        (both(has_prev, has_outer), {"tm": tm - 1, "rows": outer}),
        (both(has_next, has_outer), {"tm": tm + 1, "rows": outer}),
    )
    for there, target in greetings:
        @when(there)
        def _(target=target):
            pl.semaphore_signal(barrier, inc=1, device_id=target, device_id_type=MESH)

    def x_copy(frame):
        return pltpu.make_async_copy(x_hbm.at[frame], x_ref.at[frame], x_sem.at[frame])

    def weights(layer):
        return pltpu.make_async_copy(w_hbm.at[layer], w_raw.at[layer], w_sem.at[layer])

    gains_copy = pltpu.make_async_copy(gains_hbm, gains_ref, small_sem.at[0])
    biases_copy = pltpu.make_async_copy(biases_hbm, biases_ref, small_sem.at[1])
    gains_copy.start()
    for frame in range(frames - 1, -1, -1):
        x_copy(frame).start()
    biases_copy.start()

    def tm_row(j):
        return jnp.where(odd, 1 + j, last_row - j)

    def tm_copy(layer, at, j):
        return pltpu.make_async_remote_copy(
            src_ref=act.at[layer, frames + at, tm_row(j), 1],
            dst_ref=act.at[layer, at, tm_row(j), 1],
            send_sem=tm_send.at[layer, at, j],
            recv_sem=tm_recv.at[layer, at, j],
            device_id={"tm": tm + 1},
            device_id_type=MESH,
        )

    def corner_copy(layer, at):
        return pltpu.make_async_remote_copy(
            src_ref=act.at[layer, frames + at, edge_src[OUTER], 1],
            dst_ref=act.at[layer, at, edge_dst[OUTER], 1],
            send_sem=corner_send.at[layer, at],
            recv_sem=row_recv.at[layer, at, OUTER],
            device_id={"tm": tm + 1, "rows": outer},
            device_id_type=MESH,
        )

    def row_copy(layer, padded, side):
        return pltpu.make_async_remote_copy(
            src_ref=act.at[layer, padded, edge_src[side], 1],
            dst_ref=act.at[layer, padded, edge_dst[side], 1],
            send_sem=row_send.at[layer, padded, side],
            recv_sem=row_recv.at[layer, padded, side],
            device_id=side_target[side],
            device_id_type=MESH,
        )

    def kind(layer):
        return 0 if layer == 0 else 2 if layer == layers - 1 else 1

    def send_frame(layer, frame):
        at = frame - (frames - 2)
        for side in (OUTER, INNER):
            @when(side_there[side])
            def _(side=side):
                row_copy(layer, frame + 2, side).start()
        if at >= 0:
            before = min(CORNER_AFTER[kind(layer)][at], rows_here)

            @pl.when(has_next)
            def _():
                for j in range(before):
                    tm_copy(layer, at, j).start()

            @when(both(has_next, has_outer))
            def _():
                corner_copy(layer, at).start()

            if before < rows_here:
                @pl.when(has_next)
                def _():
                    for j in range(before, rows_here):
                        tm_copy(layer, at, j).start()

    def relay(layer, at):
        @pl.when(has_prev)
        def _():
            tm_copy(layer, at, 0).wait_recv()

        @when(both(has_prev, has_inner))
        def _():
            row_copy(layer, at, INNER).start()

    def arrive_tm(layer, at):
        @pl.when(has_prev)
        def _():
            for j in range(1, rows_here):
                tm_copy(layer, at, j).wait_recv()
        for side in (INNER, OUTER):
            @when(both(has_prev, side_there[side]))
            def _(side=side):
                row_copy(layer, at, side).wait_recv()

    def arrive_rows(layer, padded):
        for side in (INNER, OUTER):
            @when(side_there[side])
            def _(side=side):
                row_copy(layer, padded, side).wait_recv()

    lane = lax.broadcasted_iota(jnp.int32, (channels, columns), 1)
    not_first, not_last = lane > 0, lane < columns - 1

    def shift(layer, padded, h):
        line = act[layer, padded, h, 1].astype(jnp.float32)
        left = jnp.where(not_first, pltpu.roll(line, 1, 1), 0.0)
        right = jnp.where(not_last, pltpu.roll(line, columns - 1, 1), 0.0)
        act[layer, padded, h, 0] = left.astype(jnp.bfloat16)
        act[layer, padded, h, 2] = right.astype(jnp.bfloat16)

    def activate(layer, frame, value):
        squares = jnp.mean(value * value, axis=1, keepdims=True)
        half = value * lax.rsqrt(squares + EPSILON) * gain_col[layer][None]
        act[layer, frame + 2, pl.ds(1, rows_here), 1] = (
            half + half * jnp.tanh(half)
        ).astype(jnp.bfloat16)

    def prepare(layer):
        weights(layer).wait()
        taps = w_raw.shape[1] // 3
        order = [3 * b + c for b in ROW_TAPS for c in range(3)]
        for a in range(3):
            for first in range(0, taps, 2):
                count = min(2, taps - first)
                tiles = [w_raw[layer, taps * a + order[first + n]] for n in range(count)]
                block = jnp.concatenate(tiles, axis=1) if count > 1 else tiles[0]
                w_cat[layer, a, :, first * channels:(first + count) * channels] = block

    def columns_of(ref, layer):
        line = ref[pl.ds(layer, 1), :]
        return jnp.transpose(jnp.broadcast_to(line, (columns, channels)))

    gains_copy.wait()
    gain_col[0] = 0.5 * columns_of(gains_ref, 0)
    for frame in range(frames - 1, -1, -1):
        if frame == frames - 1:
            x_copy(frame).wait()
        activate(0, frame, x_ref[frame].astype(jnp.float32))
        if frame == frames - 1:
            for later in range(frames - 2, -1, -1):
                x_copy(later).wait()
            for layer in range(layers):
                weights(layer).start()
            greeted = sum(jnp.int32(1) if there is True else there.astype(jnp.int32) for there, _ in greetings)
            pl.semaphore_wait(barrier, greeted)
        send_frame(0, frame)

    biases_copy.wait()
    for layer in range(layers):
        if layer > 0:
            gain_col[layer] = 0.5 * columns_of(gains_ref, layer)
        bias_col[layer] = columns_of(biases_ref, layer)

    zero_line = jnp.zeros((channels, columns), jnp.bfloat16)

    @pl.when(jnp.logical_not(has_prev))
    def _():
        for layer in range(layers):
            for at in range(2):
                for h in range(rows_here + 2):
                    act[layer, at, h, 1] = zero_line

    for side in (INNER, OUTER):
        if side_there[side] is True:
            continue

        @when(both(has_prev, jnp.logical_not(side_there[side])))
        def _(side=side):
            for layer in range(layers):
                for at in range(2):
                    act[layer, at, halo[side], 1] = zero_line

        @pl.when(jnp.logical_not(side_there[side]))
        def _(side=side):
            for layer in range(layers):
                for at in range(2, frames + 2):
                    act[layer, at, halo[side], 1] = zero_line

    for frame in range(frames):
        for h in range(1, rows_here + 1):
            shift(0, frame + 2, h)
    for layer in range(layers):
        prepare(layer)

    depth = 9 * channels

    def window(layer, padded):
        return jnp.concatenate(
            [
                jnp.concatenate(
                    [act[layer, padded, h + b].reshape(depth // 3, columns) for b in ROW_TAPS],
                    axis=0,
                )
                for h in range(rows_here)
            ],
            axis=1,
        )

    seen = {}

    def product(layer, frame, a):
        part = jnp.dot(
            w_cat[layer, a], window(layer, frame + a), preferred_element_type=jnp.float32
        )
        if seen.get((layer, frame), 0) > 0:
            part = acc[layer, frame] + part
        seen[layer, frame] = seen.get((layer, frame), 0) + 1
        return part

    def finish(layer, frame, total):
        before = x_ref if layer == 0 else values
        results = []
        for h in range(rows_here):
            part = total[:, h * columns:(h + 1) * columns]
            summed = before[frame, h].astype(jnp.float32) + part + bias_col[layer]
            results.append(summed.astype(jnp.bfloat16))
        into = out_ref if layer == layers - 1 else values
        for h in range(rows_here):
            into[frame, h] = results[h]
        if layer < layers - 1:
            activate(layer + 1, frame, jnp.stack(results).astype(jnp.float32))

    def pass_on(layer, frames_done):
        if layer < layers - 1:
            for frame in frames_done:
                for h in range(1, rows_here + 1):
                    shift(layer + 1, frame + 2, h)
                send_frame(layer + 1, frame)

    def last_relay_sent(layer, at):
        @when(both(has_prev, has_inner))
        def _():
            row_copy(layer, at, INNER).wait_send()

    def wait_sends():
        for layer in range(layers):
            for at in range(2):
                @pl.when(has_next)
                def _(layer=layer, at=at):
                    for j in range(rows_here):
                        tm_copy(layer, at, j).wait_send()

                @when(both(has_next, has_outer))
                def _(layer=layer, at=at):
                    corner_copy(layer, at).wait_send()

                if (layer, at) != (layers - 1, 0):
                    last_relay_sent(layer, at)
            for side in (INNER, OUTER):
                @when(side_there[side])
                def _(layer=layer, side=side):
                    for padded in range(2, frames + 2):
                        row_copy(layer, padded, side).wait_send()

    for layer in range(layers):
        order = list(range(frames - 1, 0, -1)) + list(LAST_SOURCES[kind(layer)])
        for source in order:
            for at in (1, 0):
                if min(RELAY_BEFORE[kind(layer)][at], frames - 1) == source:
                    relay(layer, at)
            padded = source + 2
            if layer == layers - 1 and source == -2:
                wait_sends()
            if source >= 0:
                arrive_rows(layer, padded)
                for h in (0, last_row + 1):
                    shift(layer, padded, h)
            else:
                arrive_tm(layer, padded)
                for h in range(rows_here + 2):
                    shift(layer, padded, h)
            touched = [f for f in (source + 2, source + 1, source) if 0 <= f < frames]
            done = [f for f in touched if seen.get((layer, f), 0) == 2]
            for frame in done:
                finish(layer, frame, product(layer, frame, padded - frame))
            apart = len(done) < len(touched) and source in SENT_FIRST[kind(layer)]
            if apart:
                pass_on(layer, done)
            for frame in touched:
                if frame not in done:
                    acc[layer, frame] = product(layer, frame, padded - frame)
            if not apart:
                pass_on(layer, done)
    last_relay_sent(layers - 1, 0)


def on_device(latents, conv_weight, norm_gains, biases):
    frames, rows_here, channels, columns = latents.shape
    layers, taps = conv_weight.shape[:2]
    hbm = pl.BlockSpec(memory_space=pl.ANY)
    dma = pltpu.SemaphoreType.DMA
    return pl.pallas_call(
        functools.partial(stack_kernel, layers, frames, rows_here, channels, columns),
        out_shape=pltpu.VMEM(latents.shape, latents.dtype),
        in_specs=[hbm, hbm, hbm, hbm],
        out_specs=pl.BlockSpec(memory_space=pltpu.VMEM),
        scratch_shapes=[
            pltpu.VMEM(latents.shape, jnp.bfloat16),
            pltpu.VMEM((layers, taps, channels, channels), jnp.bfloat16),
            pltpu.VMEM((layers, 3, channels, 9 * channels), jnp.bfloat16),
            pltpu.VMEM((layers, frames, channels, rows_here * columns), jnp.float32),
            pltpu.VMEM((layers, frames + 2, rows_here + 2, 3, channels, columns), jnp.bfloat16),
            pltpu.VMEM(latents.shape, jnp.bfloat16),
            pltpu.VMEM((layers, channels), jnp.float32),
            pltpu.VMEM((layers, channels), jnp.float32),
            pltpu.VMEM((layers, channels, columns), jnp.float32),
            pltpu.VMEM((layers, channels, columns), jnp.float32),
            dma((frames,)),
            dma((layers,)),
            dma((2,)),
            dma((layers, frames + 2, 2)),
            dma((layers, frames + 2, 2)),
            dma((layers, 2, rows_here)),
            dma((layers, 2, rows_here)),
            dma((layers, 2)),
        ],
        compiler_params=pltpu.CompilerParams(
            collective_id=0, has_side_effects=True, vmem_limit_bytes=60 * 1024 * 1024
        ),
        name="conv_stack",
    )(latents, conv_weight, norm_gains, biases)


def solution(mesh):
    in_specs = (P(("clips", "tm"), "rows", None, None), P(), P(), P())
    out_specs = P(("clips", "tm"), "rows", None, None)
    return jax.shard_map(
        on_device, mesh=mesh, in_specs=in_specs, out_specs=out_specs, check_vma=False
    )
```

```python
import functools

import jax
import jax.numpy as jnp
from jax import lax
from jax.experimental import pallas as pl
from jax.experimental.pallas import tpu as pltpu
from jax.sharding import PartitionSpec as P

EPSILON = 1e-06
MESH = pl.DeviceIdType.MESH
INNER, OUTER = 0, 1
ROW_TAPS = (1, 0, 2)
CORNER_AFTER = ((1, 1), (1, 1), (1, 1))
RELAY_BEFORE = ((-2, 1), (-1, 1), (-1, 2))
LAST_SOURCES = ((0, -1, -2), (0, -1, -2), (-1, 0, -2))
SENT_FIRST = ((), (), ())


def stack_kernel(
    layers, frames, rows_here, channels, columns,
    x_hbm, w_hbm, gains_hbm, biases_hbm, out_ref,
    x_ref, w_raw, w_cat, acc, act, values, gains_ref, biases_ref, gain_col, bias_col,
    x_sem, w_sem, small_sem,
    row_send, row_recv, tm_send, tm_recv, corner_send,
):
    tm, tm_count = lax.axis_index("tm"), lax.axis_size("tm")
    row, row_count = lax.axis_index("rows"), lax.axis_size("rows")
    odd = lax.rem(row, 2) == 1
    step = jnp.where(odd, 1, -1)
    inner, outer = row - step, row + step
    has_prev, has_next = tm > 0, tm < tm_count - 1
    has_inner = True if row_count % 2 == 0 else inner < row_count
    has_outer = jnp.logical_and(outer >= 0, outer < row_count)
    last_row = rows_here
    edge_src = (jnp.where(odd, 1, last_row), jnp.where(odd, last_row, 1))
    edge_dst = (jnp.where(odd, last_row + 1, 0), jnp.where(odd, 0, last_row + 1))
    halo = (jnp.where(odd, 0, last_row + 1), jnp.where(odd, last_row + 1, 0))
    side_there = (has_inner, has_outer)
    side_target = ({"rows": inner}, {"rows": outer})

    def both(*conditions):
        conditions = [there for there in conditions if there is not True]
        return functools.reduce(jnp.logical_and, conditions) if conditions else True

    def when(there):
        return (lambda body: body()) if there is True else pl.when(there)


    barrier = pltpu.get_barrier_semaphore()
    greetings = (
        (has_prev, {"tm": tm - 1}),
        (has_next, {"tm": tm + 1}),
        (has_inner, {"rows": inner}),
        (has_outer, {"rows": outer}),
        (both(has_prev, has_outer), {"tm": tm - 1, "rows": outer}),
        (both(has_next, has_outer), {"tm": tm + 1, "rows": outer}),
    )
    for there, target in greetings:
        @when(there)
        def _(target=target):
            pl.semaphore_signal(barrier, inc=1, device_id=target, device_id_type=MESH)

    def x_copy(frame):
        return pltpu.make_async_copy(x_hbm.at[frame], x_ref.at[frame], x_sem.at[frame])

    def weights(layer):
        return pltpu.make_async_copy(w_hbm.at[layer], w_raw.at[layer], w_sem.at[layer])

    gains_copy = pltpu.make_async_copy(gains_hbm, gains_ref, small_sem.at[0])
    biases_copy = pltpu.make_async_copy(biases_hbm, biases_ref, small_sem.at[1])
    gains_copy.start()
    for frame in range(frames - 1, -1, -1):
        x_copy(frame).start()
    biases_copy.start()

    def tm_row(j):
        return jnp.where(odd, 1 + j, last_row - j)

    def tm_copy(layer, at, j):
        return pltpu.make_async_remote_copy(
            src_ref=act.at[layer, frames + at, tm_row(j), 1],
            dst_ref=act.at[layer, at, tm_row(j), 1],
            send_sem=tm_send.at[layer, at, j],
            recv_sem=tm_recv.at[layer, at, j],
            device_id={"tm": tm + 1},
            device_id_type=MESH,
        )

    def corner_copy(layer, at):
        return pltpu.make_async_remote_copy(
            src_ref=act.at[layer, frames + at, edge_src[OUTER], 1],
            dst_ref=act.at[layer, at, edge_dst[OUTER], 1],
            send_sem=corner_send.at[layer, at],
            recv_sem=row_recv.at[layer, at, OUTER],
            device_id={"tm": tm + 1, "rows": outer},
            device_id_type=MESH,
        )

    def row_copy(layer, padded, side):
        return pltpu.make_async_remote_copy(
            src_ref=act.at[layer, padded, edge_src[side], 1],
            dst_ref=act.at[layer, padded, edge_dst[side], 1],
            send_sem=row_send.at[layer, padded, side],
            recv_sem=row_recv.at[layer, padded, side],
            device_id=side_target[side],
            device_id_type=MESH,
        )

    def kind(layer):
        return 0 if layer == 0 else 2 if layer == layers - 1 else 1

    def send_frame(layer, frame):
        at = frame - (frames - 2)
        for side in (OUTER, INNER):
            @when(side_there[side])
            def _(side=side):
                row_copy(layer, frame + 2, side).start()
        if at >= 0:
            before = min(CORNER_AFTER[kind(layer)][at], rows_here)

            @pl.when(has_next)
            def _():
                for j in range(before):
                    tm_copy(layer, at, j).start()

            @when(both(has_next, has_outer))
            def _():
                corner_copy(layer, at).start()

            if before < rows_here:
                @pl.when(has_next)
                def _():
                    for j in range(before, rows_here):
                        tm_copy(layer, at, j).start()

    def relay(layer, at):
        @pl.when(has_prev)
        def _():
            tm_copy(layer, at, 0).wait_recv()

        @when(both(has_prev, has_inner))
        def _():
            row_copy(layer, at, INNER).start()

    def arrive_tm(layer, at):
        @pl.when(has_prev)
        def _():
            for j in range(1, rows_here):
                tm_copy(layer, at, j).wait_recv()
        for side in (INNER, OUTER):
            @when(both(has_prev, side_there[side]))
            def _(side=side):
                row_copy(layer, at, side).wait_recv()

    def arrive_rows(layer, padded):
        for side in (INNER, OUTER):
            @when(side_there[side])
            def _(side=side):
                row_copy(layer, padded, side).wait_recv()

    lane = lax.broadcasted_iota(jnp.int32, (channels, columns), 1)
    not_first, not_last = lane > 0, lane < columns - 1

    def shift(layer, padded, h):
        line = act[layer, padded, h, 1].astype(jnp.float32)
        left = jnp.where(not_first, pltpu.roll(line, 1, 1), 0.0)
        right = jnp.where(not_last, pltpu.roll(line, columns - 1, 1), 0.0)
        act[layer, padded, h, 0] = left.astype(jnp.bfloat16)
        act[layer, padded, h, 2] = right.astype(jnp.bfloat16)

    def activate(layer, frame, value):
        squares = jnp.mean(value * value, axis=1, keepdims=True)
        half = value * lax.rsqrt(squares + EPSILON) * gain_col[layer][None]
        act[layer, frame + 2, pl.ds(1, rows_here), 1] = (
            half + half * jnp.tanh(half)
        ).astype(jnp.bfloat16)

    def prepare(layer):
        weights(layer).wait()
        taps = w_raw.shape[1] // 3
        order = [3 * b + c for b in ROW_TAPS for c in range(3)]
        for a in range(3):
            for first in range(0, taps, 2):
                count = min(2, taps - first)
                tiles = [w_raw[layer, taps * a + order[first + n]] for n in range(count)]
                block = jnp.concatenate(tiles, axis=1) if count > 1 else tiles[0]
                w_cat[layer, a, :, first * channels:(first + count) * channels] = block

    def columns_of(ref, layer):
        line = ref[pl.ds(layer, 1), :]
        return jnp.transpose(jnp.broadcast_to(line, (columns, channels)))

    gains_copy.wait()
    gain_col[0] = 0.5 * columns_of(gains_ref, 0)
    for frame in range(frames - 1, -1, -1):
        if frame == frames - 1:
            x_copy(frame).wait()
        activate(0, frame, x_ref[frame].astype(jnp.float32))
        if frame == frames - 1:
            for later in range(frames - 2, -1, -1):
                x_copy(later).wait()
            for layer in range(layers):
                weights(layer).start()
            greeted = sum(jnp.int32(1) if there is True else there.astype(jnp.int32) for there, _ in greetings)
            pl.semaphore_wait(barrier, greeted)
        send_frame(0, frame)

    biases_copy.wait()
    for layer in range(layers):
        if layer > 0:
            gain_col[layer] = 0.5 * columns_of(gains_ref, layer)
        bias_col[layer] = columns_of(biases_ref, layer)

    zero_line = jnp.zeros((channels, columns), jnp.bfloat16)

    @pl.when(jnp.logical_not(has_prev))
    def _():
        for layer in range(layers):
            for at in range(2):
                for h in range(rows_here + 2):
                    act[layer, at, h, 1] = zero_line

    for side in (INNER, OUTER):
        if side_there[side] is True:
            continue

        @when(both(has_prev, jnp.logical_not(side_there[side])))
        def _(side=side):
            for layer in range(layers):
                for at in range(2):
                    act[layer, at, halo[side], 1] = zero_line

        @pl.when(jnp.logical_not(side_there[side]))
        def _(side=side):
            for layer in range(layers):
                for at in range(2, frames + 2):
                    act[layer, at, halo[side], 1] = zero_line

    for frame in range(frames):
        for h in range(1, rows_here + 1):
            shift(0, frame + 2, h)
    for layer in range(layers):
        prepare(layer)

    depth = 9 * channels

    def window(layer, padded):
        return jnp.concatenate(
            [
                jnp.concatenate(
                    [act[layer, padded, h + b].reshape(depth // 3, columns) for b in ROW_TAPS],
                    axis=0,
                )
                for h in range(rows_here)
            ],
            axis=1,
        )

    seen = {}

    def product(layer, frame, a):
        part = jnp.dot(
            w_cat[layer, a], window(layer, frame + a), preferred_element_type=jnp.float32
        )
        if seen.get((layer, frame), 0) > 0:
            part = acc[layer, frame] + part
        seen[layer, frame] = seen.get((layer, frame), 0) + 1
        return part

    def finish(layer, frame, total):
        before = x_ref if layer == 0 else values
        results = []
        for h in range(rows_here):
            part = total[:, h * columns:(h + 1) * columns]
            summed = before[frame, h].astype(jnp.float32) + part + bias_col[layer]
            results.append(summed.astype(jnp.bfloat16))
        into = out_ref if layer == layers - 1 else values
        for h in range(rows_here):
            into[frame, h] = results[h]
        if layer < layers - 1:
            activate(layer + 1, frame, jnp.stack(results).astype(jnp.float32))

    def pass_on(layer, frames_done):
        if layer < layers - 1:
            for frame in frames_done:
                for h in range(1, rows_here + 1):
                    shift(layer + 1, frame + 2, h)
                send_frame(layer + 1, frame)

    def last_relay_sent(layer, at):
        @when(both(has_prev, has_inner))
        def _():
            row_copy(layer, at, INNER).wait_send()

    def wait_sends():
        for layer in range(layers):
            for at in range(2):
                @pl.when(has_next)
                def _(layer=layer, at=at):
                    for j in range(rows_here):
                        tm_copy(layer, at, j).wait_send()

                @when(both(has_next, has_outer))
                def _(layer=layer, at=at):
                    corner_copy(layer, at).wait_send()

                if (layer, at) != (layers - 1, 0):
                    last_relay_sent(layer, at)
            for side in (INNER, OUTER):
                @when(side_there[side])
                def _(layer=layer, side=side):
                    for padded in range(2, frames + 2):
                        row_copy(layer, padded, side).wait_send()

    for layer in range(layers):
        order = list(range(frames - 1, 0, -1)) + list(LAST_SOURCES[kind(layer)])
        for source in order:
            for at in (1, 0):
                if min(RELAY_BEFORE[kind(layer)][at], frames - 1) == source:
                    relay(layer, at)
            padded = source + 2
            if layer == layers - 1 and source == -2:
                wait_sends()
            if source >= 0:
                arrive_rows(layer, padded)
                for h in (0, last_row + 1):
                    shift(layer, padded, h)
            else:
                arrive_tm(layer, padded)
                for h in range(rows_here + 2):
                    shift(layer, padded, h)
            touched = [f for f in (source + 2, source + 1, source) if 0 <= f < frames]
            done = [f for f in touched if seen.get((layer, f), 0) == 2]
            for frame in done:
                finish(layer, frame, product(layer, frame, padded - frame))
            apart = len(done) < len(touched) and source in SENT_FIRST[kind(layer)]
            if apart:
                pass_on(layer, done)
            for frame in touched:
                if frame not in done:
                    acc[layer, frame] = product(layer, frame, padded - frame)
            if not apart:
                pass_on(layer, done)
    last_relay_sent(layers - 1, 0)


def on_device(latents, conv_weight, norm_gains, biases):
    frames, rows_here, channels, columns = latents.shape
    layers, taps = conv_weight.shape[:2]
    hbm = pl.BlockSpec(memory_space=pl.ANY)
    dma = pltpu.SemaphoreType.DMA
    return pl.pallas_call(
        functools.partial(stack_kernel, layers, frames, rows_here, channels, columns),
        out_shape=pltpu.VMEM(latents.shape, latents.dtype),
        in_specs=[hbm, hbm, hbm, hbm],
        out_specs=pl.BlockSpec(memory_space=pltpu.VMEM),
        scratch_shapes=[
            pltpu.VMEM(latents.shape, jnp.bfloat16),
            pltpu.VMEM((layers, taps, channels, channels), jnp.bfloat16),
            pltpu.VMEM((layers, 3, channels, 9 * channels), jnp.bfloat16),
            pltpu.VMEM((layers, frames, channels, rows_here * columns), jnp.float32),
            pltpu.VMEM((layers, frames + 2, rows_here + 2, 3, channels, columns), jnp.bfloat16),
            pltpu.VMEM(latents.shape, jnp.bfloat16),
            pltpu.VMEM((layers, channels), jnp.float32),
            pltpu.VMEM((layers, channels), jnp.float32),
            pltpu.VMEM((layers, channels, columns), jnp.float32),
            pltpu.VMEM((layers, channels, columns), jnp.float32),
            dma((frames,)),
            dma((layers,)),
            dma((2,)),
            dma((layers, frames + 2, 2)),
            dma((layers, frames + 2, 2)),
            dma((layers, 2, rows_here)),
            dma((layers, 2, rows_here)),
            dma((layers, 2)),
        ],
        compiler_params=pltpu.CompilerParams(
            collective_id=0, has_side_effects=True, vmem_limit_bytes=60 * 1024 * 1024
        ),
        name="conv_stack",
    )(latents, conv_weight, norm_gains, biases)


def solution(mesh):
    in_specs = (P(("clips", "tm"), "rows", None, None), P(), P(), P())
    out_specs = P(("clips", "tm"), "rows", None, None)
    return jax.shard_map(
        on_device, mesh=mesh, in_specs=in_specs, out_specs=out_specs, check_vma=False
    )
```

```python
import functools

import jax
import jax.numpy as jnp
from jax import lax
from jax.experimental import pallas as pl
from jax.experimental.pallas import tpu as pltpu
from jax.sharding import PartitionSpec as P

EPSILON = 1e-06
MESH = pl.DeviceIdType.MESH
INNER, OUTER = 0, 1
ROW_TAPS = (1, 0, 2)
CORNER_AFTER = ((1, 1), (1, 1), (1, 1))
RELAY_BEFORE = ((-2, 1), (-1, 1), (-1, 2))
LAST_SOURCES = ((0, -1, -2), (0, -1, -2), (-1, 0, -2))
SENT_FIRST = ((), (), ())


def stack_kernel(
    layers, frames, rows_here, channels, columns,
    x_hbm, w_hbm, gains_hbm, biases_hbm, out_ref,
    x_ref, w_raw, w_cat, acc, act, values, gains_ref, biases_ref, gain_col, bias_col,
    x_sem, w_sem, small_sem,
    row_send, row_recv, tm_send, tm_recv, corner_send,
):
    tm, tm_count = lax.axis_index("tm"), lax.axis_size("tm")
    row, row_count = lax.axis_index("rows"), lax.axis_size("rows")
    odd = lax.rem(row, 2) == 1
    step = jnp.where(odd, 1, -1)
    inner, outer = row - step, row + step
    has_prev, has_next = tm > 0, tm < tm_count - 1
    has_inner = True if row_count % 2 == 0 else inner < row_count
    has_outer = jnp.logical_and(outer >= 0, outer < row_count)
    last_row = rows_here
    edge_src = (jnp.where(odd, 1, last_row), jnp.where(odd, last_row, 1))
    edge_dst = (jnp.where(odd, last_row + 1, 0), jnp.where(odd, 0, last_row + 1))
    halo = (jnp.where(odd, 0, last_row + 1), jnp.where(odd, last_row + 1, 0))
    side_there = (has_inner, has_outer)
    side_target = ({"rows": inner}, {"rows": outer})

    def both(*conditions):
        conditions = [there for there in conditions if there is not True]
        return functools.reduce(jnp.logical_and, conditions) if conditions else True

    def when(there):
        return (lambda body: body()) if there is True else pl.when(there)


    barrier = pltpu.get_barrier_semaphore()
    greetings = (
        (has_prev, {"tm": tm - 1}),
        (has_next, {"tm": tm + 1}),
        (has_inner, {"rows": inner}),
        (has_outer, {"rows": outer}),
        (both(has_prev, has_outer), {"tm": tm - 1, "rows": outer}),
        (both(has_next, has_outer), {"tm": tm + 1, "rows": outer}),
    )
    for there, target in greetings:
        @when(there)
        def _(target=target):
            pl.semaphore_signal(barrier, inc=1, device_id=target, device_id_type=MESH)

    def x_copy(frame):
        return pltpu.make_async_copy(x_hbm.at[frame], x_ref.at[frame], x_sem.at[frame])

    def weights(layer):
        return pltpu.make_async_copy(w_hbm.at[layer], w_raw.at[layer], w_sem.at[layer])

    gains_copy = pltpu.make_async_copy(gains_hbm, gains_ref, small_sem.at[0])
    biases_copy = pltpu.make_async_copy(biases_hbm, biases_ref, small_sem.at[1])
    gains_copy.start()
    for frame in range(frames - 1, -1, -1):
        x_copy(frame).start()
    biases_copy.start()

    def tm_row(j):
        return jnp.where(odd, 1 + j, last_row - j)

    def tm_copy(layer, at, j):
        return pltpu.make_async_remote_copy(
            src_ref=act.at[layer, frames + at, tm_row(j), 1],
            dst_ref=act.at[layer, at, tm_row(j), 1],
            send_sem=tm_send.at[layer, at, j],
            recv_sem=tm_recv.at[layer, at, j],
            device_id={"tm": tm + 1},
            device_id_type=MESH,
        )

    def corner_copy(layer, at):
        return pltpu.make_async_remote_copy(
            src_ref=act.at[layer, frames + at, edge_src[OUTER], 1],
            dst_ref=act.at[layer, at, edge_dst[OUTER], 1],
            send_sem=corner_send.at[layer, at],
            recv_sem=row_recv.at[layer, at, OUTER],
            device_id={"tm": tm + 1, "rows": outer},
            device_id_type=MESH,
        )

    def row_copy(layer, padded, side):
        return pltpu.make_async_remote_copy(
            src_ref=act.at[layer, padded, edge_src[side], 1],
            dst_ref=act.at[layer, padded, edge_dst[side], 1],
            send_sem=row_send.at[layer, padded, side],
            recv_sem=row_recv.at[layer, padded, side],
            device_id=side_target[side],
            device_id_type=MESH,
        )

    def kind(layer):
        return 0 if layer == 0 else 2 if layer == layers - 1 else 1

    def send_frame(layer, frame):
        at = frame - (frames - 2)
        for side in (OUTER, INNER):
            @when(side_there[side])
            def _(side=side):
                row_copy(layer, frame + 2, side).start()
        if at >= 0:
            before = min(CORNER_AFTER[kind(layer)][at], rows_here)

            @pl.when(has_next)
            def _():
                for j in range(before):
                    tm_copy(layer, at, j).start()

            @when(both(has_next, has_outer))
            def _():
                corner_copy(layer, at).start()

            if before < rows_here:
                @pl.when(has_next)
                def _():
                    for j in range(before, rows_here):
                        tm_copy(layer, at, j).start()

    def relay(layer, at):
        @pl.when(has_prev)
        def _():
            tm_copy(layer, at, 0).wait_recv()

        @when(both(has_prev, has_inner))
        def _():
            row_copy(layer, at, INNER).start()

    def arrive_tm(layer, at):
        @pl.when(has_prev)
        def _():
            for j in range(1, rows_here):
                tm_copy(layer, at, j).wait_recv()
        for side in (INNER, OUTER):
            @when(both(has_prev, side_there[side]))
            def _(side=side):
                row_copy(layer, at, side).wait_recv()

    def arrive_rows(layer, padded):
        for side in (INNER, OUTER):
            @when(side_there[side])
            def _(side=side):
                row_copy(layer, padded, side).wait_recv()

    lane = lax.broadcasted_iota(jnp.int32, (channels, columns), 1)
    not_first, not_last = lane > 0, lane < columns - 1

    def shift(layer, padded, h):
        line = act[layer, padded, h, 1].astype(jnp.float32)
        left = jnp.where(not_first, pltpu.roll(line, 1, 1), 0.0)
        right = jnp.where(not_last, pltpu.roll(line, columns - 1, 1), 0.0)
        act[layer, padded, h, 0] = left.astype(jnp.bfloat16)
        act[layer, padded, h, 2] = right.astype(jnp.bfloat16)

    def activate(layer, frame, value):
        squares = jnp.mean(value * value, axis=1, keepdims=True)
        half = value * lax.rsqrt(squares + EPSILON) * gain_col[layer][None]
        act[layer, frame + 2, pl.ds(1, rows_here), 1] = (
            half + half * jnp.tanh(half)
        ).astype(jnp.bfloat16)

    def prepare(layer):
        weights(layer).wait()
        taps = w_raw.shape[1] // 3
        order = [3 * b + c for b in ROW_TAPS for c in range(3)]
        for a in range(3):
            for first in range(0, taps, 2):
                count = min(2, taps - first)
                tiles = [w_raw[layer, taps * a + order[first + n]] for n in range(count)]
                block = jnp.concatenate(tiles, axis=1) if count > 1 else tiles[0]
                w_cat[layer, a, :, first * channels:(first + count) * channels] = block

    def columns_of(ref, layer):
        line = ref[pl.ds(layer, 1), :]
        return jnp.transpose(jnp.broadcast_to(line, (columns, channels)))

    gains_copy.wait()
    gain_col[0] = 0.5 * columns_of(gains_ref, 0)
    for frame in range(frames - 1, -1, -1):
        if frame == frames - 1:
            x_copy(frame).wait()
        activate(0, frame, x_ref[frame].astype(jnp.float32))
        if frame == frames - 1:
            for later in range(frames - 2, -1, -1):
                x_copy(later).wait()
            for layer in range(layers):
                weights(layer).start()
            greeted = sum(jnp.int32(1) if there is True else there.astype(jnp.int32) for there, _ in greetings)
            pl.semaphore_wait(barrier, greeted)
        send_frame(0, frame)
        for h in range(1, rows_here + 1):
            shift(0, frame + 2, h)

    biases_copy.wait()
    for layer in range(layers):
        if layer > 0:
            gain_col[layer] = 0.5 * columns_of(gains_ref, layer)
        bias_col[layer] = columns_of(biases_ref, layer)

    zero_line = jnp.zeros((channels, columns), jnp.bfloat16)

    @pl.when(jnp.logical_not(has_prev))
    def _():
        for layer in range(layers):
            for at in range(2):
                for h in range(rows_here + 2):
                    act[layer, at, h, 1] = zero_line

    for side in (INNER, OUTER):
        if side_there[side] is True:
            continue

        @when(both(has_prev, jnp.logical_not(side_there[side])))
        def _(side=side):
            for layer in range(layers):
                for at in range(2):
                    act[layer, at, halo[side], 1] = zero_line

        @pl.when(jnp.logical_not(side_there[side]))
        def _(side=side):
            for layer in range(layers):
                for at in range(2, frames + 2):
                    act[layer, at, halo[side], 1] = zero_line

    for layer in range(layers):
        prepare(layer)

    depth = 9 * channels

    def window(layer, padded):
        return jnp.concatenate(
            [
                jnp.concatenate(
                    [act[layer, padded, h + b].reshape(depth // 3, columns) for b in ROW_TAPS],
                    axis=0,
                )
                for h in range(rows_here)
            ],
            axis=1,
        )

    seen = {}

    def product(layer, frame, a):
        part = jnp.dot(
            w_cat[layer, a], window(layer, frame + a), preferred_element_type=jnp.float32
        )
        if seen.get((layer, frame), 0) > 0:
            part = acc[layer, frame] + part
        seen[layer, frame] = seen.get((layer, frame), 0) + 1
        return part

    def finish(layer, frame, total):
        before = x_ref if layer == 0 else values
        results = []
        for h in range(rows_here):
            part = total[:, h * columns:(h + 1) * columns]
            summed = before[frame, h].astype(jnp.float32) + part + bias_col[layer]
            results.append(summed.astype(jnp.bfloat16))
        into = out_ref if layer == layers - 1 else values
        for h in range(rows_here):
            into[frame, h] = results[h]
        if layer < layers - 1:
            activate(layer + 1, frame, jnp.stack(results).astype(jnp.float32))

    def pass_on(layer, frames_done):
        if layer < layers - 1:
            for frame in frames_done:
                for h in range(1, rows_here + 1):
                    shift(layer + 1, frame + 2, h)
                send_frame(layer + 1, frame)

    def last_relay_sent(layer, at):
        @when(both(has_prev, has_inner))
        def _():
            row_copy(layer, at, INNER).wait_send()

    def wait_sends():
        for layer in range(layers):
            for at in range(2):
                @pl.when(has_next)
                def _(layer=layer, at=at):
                    for j in range(rows_here):
                        tm_copy(layer, at, j).wait_send()

                @when(both(has_next, has_outer))
                def _(layer=layer, at=at):
                    corner_copy(layer, at).wait_send()

                if (layer, at) != (layers - 1, 0):
                    last_relay_sent(layer, at)
            for side in (INNER, OUTER):
                @when(side_there[side])
                def _(layer=layer, side=side):
                    for padded in range(2, frames + 2):
                        row_copy(layer, padded, side).wait_send()

    for layer in range(layers):
        order = list(range(frames - 1, 0, -1)) + list(LAST_SOURCES[kind(layer)])
        for source in order:
            for at in (1, 0):
                if min(RELAY_BEFORE[kind(layer)][at], frames - 1) == source:
                    relay(layer, at)
            padded = source + 2
            if layer == layers - 1 and source == -2:
                wait_sends()
            if source >= 0:
                arrive_rows(layer, padded)
                for h in (0, last_row + 1):
                    shift(layer, padded, h)
            else:
                arrive_tm(layer, padded)
                for h in range(rows_here + 2):
                    shift(layer, padded, h)
            touched = [f for f in (source + 2, source + 1, source) if 0 <= f < frames]
            done = [f for f in touched if seen.get((layer, f), 0) == 2]
            for frame in done:
                finish(layer, frame, product(layer, frame, padded - frame))
            apart = len(done) < len(touched) and source in SENT_FIRST[kind(layer)]
            if apart:
                pass_on(layer, done)
            for frame in touched:
                if frame not in done:
                    acc[layer, frame] = product(layer, frame, padded - frame)
            if not apart:
                pass_on(layer, done)
    last_relay_sent(layers - 1, 0)


def on_device(latents, conv_weight, norm_gains, biases):
    frames, rows_here, channels, columns = latents.shape
    layers, taps = conv_weight.shape[:2]
    hbm = pl.BlockSpec(memory_space=pl.ANY)
    dma = pltpu.SemaphoreType.DMA
    return pl.pallas_call(
        functools.partial(stack_kernel, layers, frames, rows_here, channels, columns),
        out_shape=pltpu.VMEM(latents.shape, latents.dtype),
        in_specs=[hbm, hbm, hbm, hbm],
        out_specs=pl.BlockSpec(memory_space=pltpu.VMEM),
        scratch_shapes=[
            pltpu.VMEM(latents.shape, jnp.bfloat16),
            pltpu.VMEM((layers, taps, channels, channels), jnp.bfloat16),
            pltpu.VMEM((layers, 3, channels, 9 * channels), jnp.bfloat16),
            pltpu.VMEM((layers, frames, channels, rows_here * columns), jnp.float32),
            pltpu.VMEM((layers, frames + 2, rows_here + 2, 3, channels, columns), jnp.bfloat16),
            pltpu.VMEM(latents.shape, jnp.bfloat16),
            pltpu.VMEM((layers, channels), jnp.float32),
            pltpu.VMEM((layers, channels), jnp.float32),
            pltpu.VMEM((layers, channels, columns), jnp.float32),
            pltpu.VMEM((layers, channels, columns), jnp.float32),
            dma((frames,)),
            dma((layers,)),
            dma((2,)),
            dma((layers, frames + 2, 2)),
            dma((layers, frames + 2, 2)),
            dma((layers, 2, rows_here)),
            dma((layers, 2, rows_here)),
            dma((layers, 2)),
        ],
        compiler_params=pltpu.CompilerParams(
            collective_id=0, has_side_effects=True, vmem_limit_bytes=60 * 1024 * 1024
        ),
        name="conv_stack",
    )(latents, conv_weight, norm_gains, biases)


def solution(mesh):
    in_specs = (P(("clips", "tm"), "rows", None, None), P(), P(), P())
    out_specs = P(("clips", "tm"), "rows", None, None)
    return jax.shard_map(
        on_device, mesh=mesh, in_specs=in_specs, out_specs=out_specs, check_vma=False
    )
```
